128 devices in a mesh: row: 8 (over z, x_lo), col: 16 (over x_hi, y, core).
Axes of the slice: x: 4 (x_hi: 2, x_lo: 2; x = x_hi * 2 + x_lo), y: 4, z: 4, core: 2. Of those that a mesh axis runs over, the one named last changes fastest.
Arguments:
- blocks: bfloat16 [8, 16, 192, 128, 128], P('row', 'col'), may hold values from -0.059814453 to 0.059814453
- block_rows: int32 [8, 16, 192], P('row', 'col'), may hold values from 0 to 255, as said below
- block_cols: int32 [8, 16, 192], P('row', 'col'), may hold values from 0 to 255, as said below
- counts: int32 [8, 16], P('row', 'col'), may hold values from 96 to 192, as said below
- travel_times: float32 [16, 262144], P(None, ('row', 'col')), may hold values from -6 to 6
Outputs:
- solution: float32 [16, 16, 8, 4096], P(None, 'col', 'row')
- scaled_direction: float32 [16, 16, 8, 4096], P(None, 'col', 'row')
The draws below stay inside these ranges and needn't reach their ends.
Inputs may be any that keep to these rules, and one draw needn't show every extreme that they name: Ray block of a slot within the 256 ray blocks of its row group; among the filled slots of one device the (block_rows, block_cols) pairs are all different. `block_cols`: cell block of a slot within the 256 cell blocks of its column group. `counts`: some device fills all 192 slots.
All inputs are finite; a program needn't handle non-finite values.
Results may differ from the reference program's by a relative error of at most 0.0054.
Values may be sent and summed in bfloat16 or wider, within the bound.
No kernel may reach another device: no remote copies, remote signals or barrier semaphores. Data moves between devices by JAX's collectives and lax.ppermute only.
A program may use at most 64 MiB of HBM per device.

```python
import jax
import jax.numpy as jnp
from jax import lax

BS = 128
RB_DEV = 256
CB_DEV = 256
NB_DEV = 192
RHS = 16
ITERS = 2
ROWS = 262144
CELLS = 524288
CELL_DEV = 4096
N_ROW = 8
N_COL = 16


def pattern_pairs(key):
    subkeys = jax.random.split(jax.random.fold_in(key, 11), N_ROW * N_COL)
    chosen = jax.vmap(lambda subkey: jax.random.permutation(subkey, RB_DEV * CB_DEV))(subkeys)[:, :NB_DEV]
    return chosen.reshape(N_ROW, N_COL, NB_DEV).astype(jnp.int32)


def draw_block_rows(key, part):
    return pattern_pairs(key) // CB_DEV


def draw_block_cols(key, part):
    return pattern_pairs(key) % CB_DEV


def draw_counts(key, part):
    first_key, second_key = jax.random.split(jax.random.fold_in(key, 23))
    base = jax.random.randint(first_key, (N_ROW * N_COL,), NB_DEV // 2, NB_DEV + 1)
    fullest = jax.random.randint(second_key, (), 0, N_ROW * N_COL)
    places = jnp.arange(N_ROW * N_COL, dtype=jnp.int32)
    filled = jnp.where(places == fullest, NB_DEV, base)
    return filled.reshape(N_ROW, N_COL).astype(jnp.int32)


def levels(stream_key, extent, cuts, smallest, high):
    gain, own = 1.0, jax.random.fold_in(stream_key, 6)
    for axis_at, blocks in cuts:
        heights = jnp.exp(jax.random.uniform(jax.random.fold_in(own, axis_at), (blocks,), jnp.float32, smallest / len(cuts), high / len(cuts)))
        gain = gain * jnp.repeat(heights, extent[axis_at] // blocks).reshape([-1 if axis == axis_at else 1 for axis in range(len(extent))])
    return gain


def centred(key, shape, scale, limit, cuts=(), held_as=jnp.bfloat16):
    factor_of = levels(key, shape, cuts, -0.22, 0.18) if cuts else 1.0
    drawn = jax.random.normal(key, shape, jnp.float32) * scale * factor_of
    return jnp.minimum(jnp.maximum(drawn, -limit), limit).astype(held_as)


def setup_inputs(seed: int = 0) -> dict:
    key_list = jax.random.split(jax.random.key(seed), 6)
    return {
        "blocks": centred(key_list[0], (N_ROW, N_COL, NB_DEV, BS, BS), 0.01, 0.059814453, ((0, 8), (1, 16))),
        "block_rows": draw_block_rows(jax.random.fold_in(key_list[5], 71), 0),
        "block_cols": draw_block_cols(jax.random.fold_in(key_list[5], 71), 0),
        "counts": draw_counts(jax.random.fold_in(key_list[5], 71), 0),
        "travel_times": centred(key_list[4], (RHS, ROWS), 1.0, 6.0, ((1, 128),), jnp.float32),
    }


norm_eps = 1e-06

def rotation(rho_bar, phi_bar, beta_norm, alpha_norm):
    rho_new = jnp.sqrt(rho_bar * rho_bar + beta_norm * beta_norm)
    cosine = rho_bar / rho_new
    sine_val = beta_norm / rho_new
    theta_coef = sine_val * alpha_norm
    rho_next = -cosine * alpha_norm
    phi_new = cosine * phi_bar
    phi_next = sine_val * phi_bar
    return (phi_new / rho_new, theta_coef / rho_new, rho_next, phi_next)

def flat_inputs(blocks, block_rows, block_cols, counts):
    device_ids = jnp.arange(N_ROW * N_COL, dtype=jnp.int32)
    return (device_ids, blocks.reshape(N_ROW * N_COL, NB_DEV, BS, BS), block_rows.reshape(N_ROW * N_COL, NB_DEV), block_cols.reshape(N_ROW * N_COL, NB_DEV), counts.reshape(N_ROW * N_COL))

def hot_table(indices, count_here, width):
    filled = jnp.arange(NB_DEV, dtype=jnp.int32) < count_here
    return ((indices[None, :] == jnp.arange(width, dtype=jnp.int32)[:, None]) & filled[None, :]).astype(jnp.float32)

def apply_forward(items_all, right_full):
    count_rhs = right_full.shape[0]

    def visit(total, items):
        device_id, blocks_here, rows_here, cols_here, count_here = items
        row_group = device_id // N_COL
        col_group = device_id % N_COL
        segment = lax.dynamic_slice_in_dim(right_full, col_group * (CB_DEV * BS), CB_DEV * BS, 1)
        picked = jnp.take(segment.reshape(count_rhs, CB_DEV, BS), cols_here, axis=1)
        product = jnp.einsum('knj,nij->kni', picked.astype(jnp.float32), blocks_here.astype(jnp.float32), precision=lax.Precision.HIGHEST)
        row_hot = hot_table(rows_here, count_here, RB_DEV)
        part = jnp.einsum('rn,kni->kri', row_hot, product, precision=lax.Precision.HIGHEST).reshape(count_rhs, RB_DEV * BS)
        start = row_group * (RB_DEV * BS)
        current = lax.dynamic_slice_in_dim(total, start, RB_DEV * BS, 1)
        return (lax.dynamic_update_slice_in_dim(total, current + part, start, 1), None)
    return lax.scan(visit, jnp.zeros((count_rhs, ROWS), jnp.float32), items_all)[0]

def apply_backward(items_all, left_full):
    count_rhs = left_full.shape[0]

    def visit(total, items):
        device_id, blocks_here, rows_here, cols_here, count_here = items
        row_group = device_id // N_COL
        col_group = device_id % N_COL
        segment = lax.dynamic_slice_in_dim(left_full, row_group * (RB_DEV * BS), RB_DEV * BS, 1)
        picked = jnp.take(segment.reshape(count_rhs, RB_DEV, BS), rows_here, axis=1)
        product = jnp.einsum('kni,nij->knj', picked.astype(jnp.float32), blocks_here.astype(jnp.float32), precision=lax.Precision.HIGHEST)
        col_hot = hot_table(cols_here, count_here, CB_DEV)
        part = jnp.einsum('cn,knj->kcj', col_hot, product, precision=lax.Precision.HIGHEST).reshape(count_rhs, CB_DEV * BS)
        start = col_group * (CB_DEV * BS)
        current = lax.dynamic_slice_in_dim(total, start, CB_DEV * BS, 1)
        return (lax.dynamic_update_slice_in_dim(total, current + part, start, 1), None)
    return lax.scan(visit, jnp.zeros((count_rhs, CELLS), jnp.float32), items_all)[0]

def vector_norm(values):
    return jnp.sqrt(lax.optimization_barrier(jnp.sum(values * values, axis=1)) + norm_eps)

def reference(blocks, block_rows, block_cols, counts, travel_times):
    items_all = flat_inputs(blocks, block_rows, block_cols, counts)
    beta_norm = vector_norm(travel_times)
    left_vec = travel_times / beta_norm[:, None]
    cells_vec = apply_backward(items_all, left_vec.astype(jnp.bfloat16))
    alpha_norm = vector_norm(cells_vec)
    right_vec = cells_vec / alpha_norm[:, None]
    direction = right_vec
    solution = jnp.zeros_like(right_vec)
    phi_bar = beta_norm
    rho_bar = alpha_norm
    for iteration in range(ITERS):
        rays_vec = apply_forward(items_all, right_vec.astype(jnp.bfloat16)) - alpha_norm[:, None] * left_vec
        beta_norm = vector_norm(rays_vec)
        left_vec = rays_vec / beta_norm[:, None]
        cells_vec = apply_backward(items_all, left_vec.astype(jnp.bfloat16)) - beta_norm[:, None] * right_vec
        alpha_norm = vector_norm(cells_vec)
        right_vec = cells_vec / alpha_norm[:, None]
        step_scale, turn_scale, rho_bar, phi_bar = rotation(rho_bar, phi_bar, beta_norm, alpha_norm)
        solution = solution + step_scale[:, None] * direction
        direction = right_vec - turn_scale[:, None] * direction
    count_rhs = travel_times.shape[0]
    scaled = phi_bar[:, None] * direction
    return (solution.reshape(count_rhs, N_COL, N_ROW, CELL_DEV), scaled.reshape(count_rhs, N_COL, N_ROW, CELL_DEV))
```

```python
import functools

import jax
import jax.numpy as jnp
from jax import lax
from jax.experimental import pallas as pl
from jax.experimental.pallas import tpu as pltpu
from jax.sharding import Mesh, PartitionSpec as P

ITERS = 2
LANES = 128
NORM_EPS = 1e-06
SQUARES_FLOOR = 1e-30
CELL_GAIN = 4096.0
RAY_GAIN = 2048.0
CHUNK = 16
CHIPS_OF_COL = ("xh", "y")
DEVICES_OF_ROW = ("z", "xl")
VMEM_BYTES = 24 << 20


def exponent_of(squares):
    return jnp.ceil(jnp.log2(jnp.maximum(squares, SQUARES_FLOOR)))


def side_lanes(lane, first, second, third):
    return jnp.where(lane == 0, first, jnp.where(lane == 1, second, jnp.where(lane == 2, third, 0.0)))


def side_of_squares(squares, lane):
    exponent = exponent_of(squares)
    fraction = squares * jnp.exp2(-exponent)
    upper = jnp.floor(fraction * 1024.0)
    return side_lanes(lane, exponent, upper, fraction * 1024.0 - upper), exponent


def squares_of_side(side):
    exponent = side[:, :, 0]
    return exponent, (side[:, :, 1] + side[:, :, 2]) * (1.0 / 1024.0) * jnp.exp2(exponent)


def fetch(chunk, blocks_hbm, held, sems):
    piece = pl.ds(chunk * CHUNK, CHUNK)
    return pltpu.make_async_copy(blocks_hbm.at[piece], held.at[piece], sems.at[chunk])


def products(count, blocks_hbm, held, sems, prepare, step):
    chunks = (count + (CHUNK - 1)) // CHUNK

    def begin(chunk, carry):
        fetch(chunk, blocks_hbm, held, sems).start()
        return carry

    def visit(chunk, carry):
        fetch(chunk, blocks_hbm, held, sems).wait()
        for at in range(CHUNK):
            step(chunk * CHUNK + at)
        return carry

    lax.fori_loop(0, chunks, begin, 0)
    prepare()
    lax.fori_loop(0, chunks, visit, 0)


def rays_kernel(rows, cols, scalars, right, blocks_hbm, keep, send, total, held, sems):
    count, core = scalars[0], scalars[1]
    half = keep.shape[0]

    def prepare():
        total[...] = jnp.zeros_like(total)
        side = sum(right[33 * at + 32].astype(jnp.float32) for at in range(8))
        squares = jnp.broadcast_to(jnp.sum(side, axis=1, keepdims=True), side.shape)
        for at in range(16):
            total[17 * at + 16] = squares

    def step(slot):
        row, col = rows[slot], cols[slot]
        picked = right[col + (col >> 5)]
        product = lax.dot_general(
            picked, held[slot], (((1,), (1,)), ((), ())), preferred_element_type=jnp.float32
        )
        place = (((row >> 4) & 1) ^ core) * half + (row >> 5) * 17 + (row & 15)
        total[place] += jnp.where(slot < count, product, 0.0)

    products(count, blocks_hbm, held, sems, prepare, step)
    keep[...] = total[:half]
    send[...] = total[half:]


def cells_kernel(rows, cols, scalars, left_own, left_other, blocks_hbm, out, left, held, sems):
    count, core = scalars[0], scalars[1]
    half = left_own.shape[0]
    left[pl.ds(core * half, half)] = left_own[...]
    left[pl.ds((1 - core) * half, half)] = left_other[...]
    side = sum(left[17 * at + 16].astype(jnp.float32) for at in range(16))
    squares = jnp.broadcast_to(jnp.sum(side, axis=1, keepdims=True), side.shape)
    lane = lax.broadcasted_iota(jnp.int32, side.shape, 1)
    packed, exponent = side_of_squares(squares, lane)
    scale = CELL_GAIN * jnp.exp2(-0.5 * exponent)

    def prepare():
        out[...] = jnp.zeros_like(out)
        for at in range(8):
            out[33 * at + 32] = packed

    def step(slot):
        row, col = rows[slot], cols[slot]
        picked = left[((row >> 4) & 1) * half + (row >> 5) * 17 + (row & 15)]
        product = lax.dot_general(
            picked, held[slot], (((1,), (0,)), ((), ())), preferred_element_type=jnp.float32
        )
        out[col + (col >> 5)] += jnp.where(slot < count, product * scale, 0.0)

    products(count, blocks_hbm, held, sems, prepare, step)


def kernel_call(body, outs, scratch, slots, tables, vectors, blocks):
    specs = [pl.BlockSpec(memory_space=pltpu.SMEM)] * 3
    specs += [pl.BlockSpec(memory_space=pltpu.VMEM)] * len(vectors)
    specs += [pl.BlockSpec(memory_space=pl.ANY)]
    return pl.pallas_call(
        body,
        out_shape=outs,
        in_specs=specs,
        out_specs=jax.tree.map(lambda _: pl.BlockSpec(memory_space=pltpu.VMEM), outs),
        scratch_shapes=[
            scratch,
            pltpu.VMEM((slots, LANES, LANES), jnp.bfloat16),
            pltpu.SemaphoreType.DMA((slots // CHUNK,)),
        ],
        compiler_params=pltpu.CompilerParams(vmem_limit_bytes=VMEM_BYTES),
        cost_estimate=pl.CostEstimate(
            flops=2 * slots * LANES * LANES * 16, bytes_accessed=slots * LANES * LANES * 2 + (4 << 20), transcendentals=0
        ),
    )(*tables, *vectors, blocks)


def split_squares(values):
    squares = jnp.sum(values * values, axis=(0, 2))[:, None]
    first = lax.reduce_precision(squares, 8, 7)
    second = lax.reduce_precision(squares - first, 8, 7)
    lane = lax.broadcasted_iota(jnp.int32, (squares.shape[0], LANES), 1)
    return side_lanes(lane, first, second, squares - first - second)


def spread(values, axes, copies):
    piece = jnp.concatenate([values, split_squares(values)[None]], axis=0).astype(jnp.bfloat16)
    sent = jnp.broadcast_to(piece[None], (copies,) + piece.shape)
    got = lax.all_to_all(sent, axes, 0, 0, tiled=True)
    return got.reshape((-1,) + piece.shape[1:])


def collect(sent, axes, sources, gain):
    got = lax.all_to_all(sent.astype(jnp.float16), axes, 0, 0, tiled=True)
    got = got.reshape((sources, -1) + sent.shape[1:]).astype(jnp.float32)
    exponent, squares = squares_of_side(got[:, -1])
    weight = jnp.exp2(0.5 * exponent) * (1.0 / gain)
    norm = jnp.sqrt(jnp.sum(squares, axis=0) + NORM_EPS)
    return jnp.sum(got[:, :-1] * weight[:, None, :, None], axis=0), norm


def swap_cores(values):
    return lax.ppermute(values, "c", [(0, 1), (1, 0)])


def rotation(rho_bar, phi_bar, beta_norm, alpha_norm):
    rho_new = jnp.sqrt(rho_bar * rho_bar + beta_norm * beta_norm)
    cosine = rho_bar / rho_new
    sine_val = beta_norm / rho_new
    theta_coef = sine_val * alpha_norm
    rho_next = -cosine * alpha_norm
    phi_new = cosine * phi_bar
    phi_next = sine_val * phi_bar
    return (phi_new / rho_new, theta_coef / rho_new, rho_next, phi_next)


def per_rhs(scale):
    return scale[None, :, None]


def shards(blocks, block_rows, block_cols, counts, travel_times):
    blocks_here = blocks[0, 0]
    slots = blocks_here.shape[0]
    core = lax.axis_index("c").astype(jnp.int32)
    tables = (block_rows[0, 0], block_cols[0, 0], jnp.stack([counts[0, 0], core]))
    count_rhs = travel_times.shape[0]
    block = (count_rhs, LANES)

    def rays_of(right_raw):
        right_full = spread(right_raw, DEVICES_OF_ROW, 8)
        keep, send = kernel_call(
            rays_kernel,
            [jax.ShapeDtypeStruct((8 * 17,) + block, jnp.float32)] * 2,
            pltpu.VMEM((16 * 17,) + block, jnp.float32),
            slots, tables, (right_full,), blocks_here,
        )
        both = (keep + swap_cores(send)).reshape((8, 17) + block)
        squares = both[0, 16, :, :1]
        packed, exponent = side_of_squares(squares, lax.broadcasted_iota(jnp.int32, block, 1))
        scale = RAY_GAIN * jnp.exp2(-0.5 * exponent)
        is_side = lax.broadcasted_iota(jnp.int32, (1, 17, 1, 1), 1) == 16
        sent = jnp.where(is_side, packed, both * scale)
        return collect(sent.reshape((8 * 17,) + block), CHIPS_OF_COL, 8, RAY_GAIN)

    def cells_of(left_raw):
        left_own = spread(left_raw, CHIPS_OF_COL, 8)
        left_other = swap_cores(left_own)
        out = kernel_call(
            cells_kernel,
            jax.ShapeDtypeStruct((8 * 33,) + block, jnp.float32),
            pltpu.VMEM((16 * 17,) + block, jnp.bfloat16),
            slots, tables, (left_own, left_other), blocks_here,
        )
        return collect(out, DEVICES_OF_ROW, 8, CELL_GAIN)

    def whole_norm(values):
        squares = jnp.sum(values * values, axis=(0, 2))
        sent = jnp.broadcast_to(jnp.pad(squares, (0, LANES - count_rhs)), (128, 8, LANES))
        got = lax.all_to_all(sent, ("z", "xl", "xh", "y", "c"), 0, 0, tiled=True)
        return jnp.sqrt(jnp.sum(got[:, 0, :count_rhs], axis=0) + NORM_EPS)

    left_raw = travel_times.reshape(count_rhs, -1, LANES).transpose(1, 0, 2)
    product, beta_norm = cells_of(left_raw)
    left = left_raw / per_rhs(beta_norm)
    right_raw = product / per_rhs(beta_norm)
    phi_bar = beta_norm
    solution, direction, rho_bar = None, None, None
    for iteration in range(ITERS):
        product, alpha_norm = rays_of(right_raw)
        right = right_raw / per_rhs(alpha_norm)
        if iteration == 0:
            direction, rho_bar = right, alpha_norm
        else:
            step_scale, turn_scale, rho_bar, phi_bar = rotation(rho_bar, phi_bar, beta_norm, alpha_norm)
            solution = per_rhs(step_scale) * direction
            direction = right - per_rhs(turn_scale) * direction
        left_raw = product / per_rhs(alpha_norm) - per_rhs(alpha_norm) * left
        product, beta_norm = cells_of(left_raw)
        left = left_raw / per_rhs(beta_norm)
        right_raw = product / per_rhs(beta_norm) - per_rhs(beta_norm) * right
    alpha_norm = whole_norm(right_raw)
    right = right_raw / per_rhs(alpha_norm)
    step_scale, turn_scale, rho_bar, phi_bar = rotation(rho_bar, phi_bar, beta_norm, alpha_norm)
    solution = solution + per_rhs(step_scale) * direction
    direction = right - per_rhs(turn_scale) * direction
    scaled = per_rhs(phi_bar) * direction

    def placed(values):
        return values.transpose(1, 0, 2).reshape(count_rhs, 1, 1, -1)

    return (placed(solution), placed(scaled))


def solution(mesh):
    physical = Mesh(mesh.devices.reshape(4, 2, 2, 4, 2), ("z", "xl", "xh", "y", "c"))
    row, col = ("z", "xl"), ("xh", "y", "c")
    placed = (
        P(row, col, None, None, None),
        P(row, col, None),
        P(row, col, None),
        P(row, col),
        P(None, row + col),
    )
    return jax.shard_map(
        shards,
        mesh=physical,
        in_specs=placed,
        out_specs=(P(None, col, row, None), P(None, col, row, None)),
        check_vma=False,
    )
```

```python
import functools

import jax
import jax.numpy as jnp
from jax import lax
from jax.experimental import pallas as pl
from jax.experimental.pallas import tpu as pltpu
from jax.sharding import Mesh, PartitionSpec as P

LANES = 128
NORM_EPS = 1e-06
SQUARES_FLOOR = 1e-30
CELL_GAIN = 4096.0
RAY_GAIN = 2048.0
CHUNK = 64
CHIPS_OF_COL = ("xh", "y")
DEVICES_OF_ROW = ("z", "xl")
VMEM_BYTES = 32 << 20


def exponent_of(squares):
    return jnp.ceil(jnp.log2(jnp.maximum(squares, SQUARES_FLOOR)))


def side_lanes(lane, first, second, third):
    return jnp.where(lane == 0, first, jnp.where(lane == 1, second, jnp.where(lane == 2, third, 0.0)))


def side_of_squares(squares, lane):
    exponent = exponent_of(squares)
    fraction = squares * jnp.exp2(-exponent)
    upper = jnp.floor(fraction * 1024.0)
    return side_lanes(lane, exponent, upper, fraction * 1024.0 - upper), exponent


def pair_products(count, vector, held, source, visit):
    def chunk(at, carry):
        for step in range(0, CHUNK, 2):
            slot = at * CHUNK + step
            picked = jnp.concatenate([vector[source(slot)], vector[source(slot + 1)]], axis=0)
            pair = jnp.concatenate([held[slot], held[slot + 1]], axis=1)
            both = lax.dot_general(picked, pair, (((1,), (0,)), ((), ())), preferred_element_type=jnp.float32)
            rhs = both.shape[0] // 2
            visit(slot, both[:rhs, :LANES])
            visit(slot + 1, both[rhs:, LANES:])
        return carry

    lax.fori_loop(0, (count + (CHUNK - 1)) // CHUNK, chunk, 0)


def rays_kernel(rows, cols, scalars, right, turned, keep, send, total):
    count, core = scalars[0], scalars[1]
    half = keep.shape[0]
    total[...] = jnp.zeros_like(total)
    side = sum(right[33 * at + 32].astype(jnp.float32) for at in range(8))
    squares = jnp.broadcast_to(jnp.sum(side, axis=1, keepdims=True), side.shape)

    def source(slot):
        col = cols[slot]
        return col + (col >> 5)

    def visit(slot, product):
        row = rows[slot]
        place = (((row >> 4) & 1) ^ core) * half + (row >> 5) * 17 + (row & 15)
        place = jnp.where(slot < count, place, 16)
        total[place] += product

    pair_products(count, right, turned, source, visit)
    for at in range(16):
        total[17 * at + 16] = squares
    keep[...] = total[:half]
    send[...] = total[half:]


def cells_kernel(turn, rows, cols, scalars, left_own, left_other, held, out, *rest):
    left = rest[-1]
    count, core = scalars[0], scalars[1]
    half = left_own.shape[0]
    left[pl.ds(core * half, half)] = left_own[...]
    left[pl.ds((1 - core) * half, half)] = left_other[...]
    out[...] = jnp.zeros_like(out)
    side = sum(left[17 * at + 16].astype(jnp.float32) for at in range(16))
    squares = jnp.broadcast_to(jnp.sum(side, axis=1, keepdims=True), side.shape)
    lane = lax.broadcasted_iota(jnp.int32, side.shape, 1)
    packed, exponent = side_of_squares(squares, lane)
    scale = CELL_GAIN * jnp.exp2(-0.5 * exponent)

    def source(slot):
        row = rows[slot]
        return ((row >> 4) & 1) * half + (row >> 5) * 17 + (row & 15)

    def visit(slot, product):
        col = cols[slot]
        place = jnp.where(slot < count, col + (col >> 5), 32)
        out[place] += product * scale
        if turn:
            rest[0][slot] = held[slot].T

    pair_products(count, left, held, source, visit)
    for at in range(8):
        out[33 * at + 32] = packed


def send_blocks(sent, values, squares):
    size = sent.shape[0] // 8
    for at, value in enumerate(values):
        rounded = value.astype(jnp.bfloat16)
        for copy in range(8):
            sent[size * copy + at] = rounded
    squares = jnp.sum(squares, axis=1, keepdims=True)
    first = squares.astype(jnp.bfloat16).astype(jnp.float32)
    second = (squares - first).astype(jnp.bfloat16).astype(jnp.float32)
    lane = lax.broadcasted_iota(jnp.int32, (squares.shape[0], LANES), 1)
    side = side_lanes(lane, first, second, squares - first - second).astype(jnp.bfloat16)
    for copy in range(8):
        sent[size * copy + size - 1] = side


def start_kernel(times, sent, raw):
    squares = jnp.zeros(raw.shape[1:], jnp.float32)
    for at in range(raw.shape[0]):
        value = times[:, LANES * at : LANES * (at + 1)]
        raw[at] = value
        squares += value * value
    send_blocks(sent, [times[:, LANES * at : LANES * (at + 1)] for at in range(raw.shape[0])], squares)


def core_kernel(keep, received, out):
    squares = keep[16] + received[16]
    lane = lax.broadcasted_iota(jnp.int32, squares.shape, 1)
    packed, exponent = side_of_squares(squares, lane)
    scale = RAY_GAIN * jnp.exp2(-0.5 * exponent)
    for chip in range(8):
        for at in range(16):
            out[17 * chip + at] = (keep[17 * chip + at] + received[17 * chip + at]) * scale
        out[17 * chip + 16] = packed


def update_kernel(gain, first, last, got, *rest):
    previous, (raw, norm_out, tail) = rest[:-3], rest[-3:]
    size = raw.shape[0] + 1
    weights, total = [], 0.0
    for source in range(8):
        side = got[size * source + size - 1]
        exponent = side[:, 0:1]
        weights.append(jnp.broadcast_to(jnp.exp2(0.5 * exponent) * (1.0 / gain), side.shape))
        total += (side[:, 1:2] + side[:, 2:3]) * (1.0 / 1024.0) * jnp.exp2(exponent)
    norm = jnp.sqrt(jnp.broadcast_to(total, raw.shape[1:]) + NORM_EPS)
    norm_out[...] = norm
    inverse = 1.0 / norm
    weights = [weight * inverse for weight in weights]
    if not first:
        past = norm / previous[1][...]
    squares = jnp.zeros(raw.shape[1:], jnp.float32)
    values = []
    for at in range(size - 1):
        value = got[at] * weights[0]
        for source in range(1, 8):
            value += got[size * source + at] * weights[source]
        if not first:
            value -= previous[0][at] * past
        raw[at] = value
        squares += value * value
        values.append(value)
    if last:
        squares = jnp.broadcast_to(jnp.sum(squares, axis=1, keepdims=True), squares.shape)
        tail[...] = jnp.sum(jnp.where(diagonal(squares.shape), squares, 0.0), axis=0, keepdims=True)
    else:
        send_blocks(tail, [raw[at] for at in range(size - 1)], squares)


def diagonal(shape):
    return lax.broadcasted_iota(jnp.int32, shape, 0) == lax.broadcasted_iota(jnp.int32, shape, 1)


def finish_kernel(sums, raw0, raw1, raw2, alpha0, alpha1, beta0, beta1, beta2, solution_out, scaled_out):
    shape = alpha0.shape
    total = jnp.broadcast_to(jnp.sum(sums[:, 0, :], axis=0, keepdims=True), shape)
    total = jnp.sum(jnp.where(diagonal(shape), total, 0.0), axis=1, keepdims=True)
    alpha2 = jnp.sqrt(jnp.broadcast_to(total, shape) + NORM_EPS)
    phi_bar, rho_bar = beta0[...], alpha0[...]
    step1, turn1, rho_bar, phi_bar = rotation(rho_bar, phi_bar, beta1[...], alpha1[...])
    step2, turn2, rho_bar, phi_bar = rotation(rho_bar, phi_bar, beta2[...], alpha2)
    over0, over1, over2 = 1.0 / alpha0[...], 1.0 / alpha1[...], 1.0 / alpha2
    for at in range(raw0.shape[0]):
        lanes = slice(LANES * at, LANES * (at + 1))
        direction0 = raw0[at] * over0
        direction1 = raw1[at] * over1 - turn1 * direction0
        direction2 = raw2[at] * over2 - turn2 * direction1
        solution_out[:, lanes] = step1 * direction0 + step2 * direction1
        scaled_out[:, lanes] = phi_bar * direction2


def small_call(body, outs, *args):
    return pl.pallas_call(
        body,
        out_shape=outs,
        in_specs=[pl.BlockSpec(memory_space=pltpu.VMEM)] * len(args),
        out_specs=[pl.BlockSpec(memory_space=pltpu.VMEM)] * len(outs),
        compiler_params=pltpu.CompilerParams(vmem_limit_bytes=VMEM_BYTES),
    )(*args)


def kernel_call(body, outs, scratch, tables, vectors, blocks):
    specs = [pl.BlockSpec(memory_space=pltpu.SMEM)] * 3
    specs += [pl.BlockSpec(memory_space=pltpu.VMEM)] * (len(vectors) + 1)
    slots = blocks.shape[0]
    return pl.pallas_call(
        body,
        out_shape=outs,
        in_specs=specs,
        out_specs=[pl.BlockSpec(memory_space=pltpu.VMEM)] * len(outs),
        scratch_shapes=[scratch],
        compiler_params=pltpu.CompilerParams(vmem_limit_bytes=VMEM_BYTES),
        cost_estimate=pl.CostEstimate(
            flops=2 * slots * LANES * LANES * 16, bytes_accessed=slots * LANES * LANES * 2 + (4 << 20), transcendentals=0
        ),
    )(*tables, *vectors, blocks)


def exchange(sent, axes):
    return lax.all_to_all(sent, axes, 0, 0, tiled=True)


def exchange_halves(sent, axes):
    return exchange(sent.astype(jnp.float16), axes).astype(jnp.float32)


def swap_cores(values):
    return lax.ppermute(values, "c", [(0, 1), (1, 0)])


def rotation(rho_bar, phi_bar, beta_norm, alpha_norm):
    rho_new = jnp.sqrt(rho_bar * rho_bar + beta_norm * beta_norm)
    cosine = rho_bar / rho_new
    sine_val = beta_norm / rho_new
    theta_coef = sine_val * alpha_norm
    rho_next = -cosine * alpha_norm
    phi_new = cosine * phi_bar
    phi_next = sine_val * phi_bar
    return (phi_new / rho_new, theta_coef / rho_new, rho_next, phi_next)


def shards(blocks, block_rows, block_cols, counts, travel_times):
    blocks_here = blocks[0, 0]
    core = lax.axis_index("c").astype(jnp.int32)
    tables = (block_rows[0, 0], block_cols[0, 0], jnp.stack([counts[0, 0], core]))
    count_rhs = travel_times.shape[0]
    block = (count_rhs, LANES)
    shape = jax.ShapeDtypeStruct
    rays_sent = shape((8 * 17,) + block, jnp.bfloat16)
    cells_sent = shape((8 * 33,) + block, jnp.bfloat16)
    one = shape(block, jnp.float32)

    def rays_of(sent, turned, left_raw, beta):
        right_full = exchange(sent, DEVICES_OF_ROW)
        keep, send = kernel_call(
            rays_kernel,
            [shape((8 * 17,) + block, jnp.float32)] * 2,
            pltpu.VMEM((16 * 17,) + block, jnp.float32),
            tables, (right_full,), turned,
        )
        (both,) = small_call(core_kernel, [shape((8 * 17,) + block, jnp.float32)], keep, swap_cores(send))
        got = exchange_halves(both, CHIPS_OF_COL)
        outs = [shape((16,) + block, jnp.float32), one, rays_sent]
        return small_call(functools.partial(update_kernel, RAY_GAIN, False, False), outs, got, left_raw, beta)

    def cells_of(sent, *previous, last=False):
        first = not previous
        left_own = exchange(sent, CHIPS_OF_COL)
        outs = [shape((8 * 33,) + block, jnp.float32)]
        if first:
            outs.append(shape(blocks_here.shape, blocks_here.dtype))
        out, *turned = kernel_call(
            functools.partial(cells_kernel, first),
            outs,
            pltpu.VMEM((16 * 17,) + block, jnp.bfloat16),
            tables, (left_own, swap_cores(left_own)), blocks_here,
        )
        got = exchange_halves(out, DEVICES_OF_ROW)
        outs = [shape((32,) + block, jnp.float32), one, shape((1, LANES), jnp.float32) if last else cells_sent]
        return (*small_call(functools.partial(update_kernel, CELL_GAIN, first, last), outs, got, *previous), *turned)

    sent, left_raw = small_call(start_kernel, [rays_sent, shape((16,) + block, jnp.float32)], travel_times)
    raw0, beta0, sent, turned = cells_of(sent)
    left_raw, alpha0, sent = rays_of(sent, turned, left_raw, beta0)
    raw1, beta1, sent = cells_of(sent, raw0, alpha0)
    left_raw, alpha1, sent = rays_of(sent, turned, left_raw, beta1)
    raw2, beta2, squares = cells_of(sent, raw1, alpha1, last=True)
    squares = squares + swap_cores(squares)
    sums = exchange(jnp.broadcast_to(squares, (64, 1, LANES)), DEVICES_OF_ROW + CHIPS_OF_COL)
    flat = shape((count_rhs, 32 * LANES), jnp.float32)
    outs = small_call(finish_kernel, [flat] * 2, sums, raw0, raw1, raw2, alpha0, alpha1, beta0, beta1, beta2)
    return tuple(out.reshape(count_rhs, 1, 1, -1) for out in outs)


def solution(mesh):
    physical = Mesh(mesh.devices.reshape(4, 2, 2, 4, 2), ("z", "xl", "xh", "y", "c"))
    row, col = ("z", "xl"), ("xh", "y", "c")
    placed = (
        P(row, col, None, None, None),
        P(row, col, None),
        P(row, col, None),
        P(row, col),
        P(None, row + col),
    )
    return jax.shard_map(
        shards,
        mesh=physical,
        in_specs=placed,
        out_specs=(P(None, col, row, None), P(None, col, row, None)),
        check_vma=False,
    )
```

```python
import functools

import jax
import jax.numpy as jnp
from jax import lax
from jax.experimental import pallas as pl
from jax.experimental.pallas import tpu as pltpu
from jax.sharding import Mesh, PartitionSpec as P

LANES = 128
NORM_EPS = 1e-06
SQUARES_FLOOR = 1e-30
CELL_GAIN = 4096.0
RAY_GAIN = 2048.0
CHUNK = 64
FIRST_CHUNK = 32
STAGGER = 7000
CHIPS_OF_COL = ("xh", "y")
DEVICES_OF_ROW = ("z", "xl")
VMEM_BYTES = 32 << 20


def exponent_of(squares):
    return jnp.ceil(jnp.log2(jnp.maximum(squares, SQUARES_FLOOR)))


def side_lanes(lane, first, second, third):
    return jnp.where(lane == 0, first, jnp.where(lane == 1, second, jnp.where(lane == 2, third, 0.0)))


def side_of_squares(squares, lane):
    exponent = exponent_of(squares)
    fraction = squares * jnp.exp2(-exponent)
    upper = jnp.floor(fraction * 1024.0)
    return side_lanes(lane, exponent, upper, fraction * 1024.0 - upper), exponent


def pair_products(count, vector, held, source, visit, width=CHUNK, arrive=None):
    chunks = (count + (width - 1)) // width

    def chunk(at, carry):
        if arrive is not None:
            arrive(at)
        for step in range(0, width, 2):
            slot = at * width + step
            picked = jnp.concatenate([vector[source(slot)], vector[source(slot + 1)]], axis=0)
            pair = jnp.concatenate([held[slot], held[slot + 1]], axis=1)
            both = lax.dot_general(picked, pair, (((1,), (0,)), ((), ())), preferred_element_type=jnp.float32)
            rhs = both.shape[0] // 2
            visit(slot, both[:rhs, :LANES])
            visit(slot + 1, both[rhs:, LANES:])
        return carry

    lax.fori_loop(0, chunks, chunk, 0)
    return chunks


def rays_kernel(rows, cols, scalars, right, turned, keep, send, total):
    count, core = scalars[0], scalars[1]
    half = keep.shape[0]
    total[...] = jnp.zeros_like(total)
    side = sum(right[33 * at + 32].astype(jnp.float32) for at in range(8))
    squares = jnp.broadcast_to(jnp.sum(side, axis=1, keepdims=True), side.shape)

    def source(slot):
        col = cols[slot]
        return col + (col >> 5)

    def visit(slot, product):
        row = rows[slot]
        place = (((row >> 4) & 1) ^ core) * half + (row >> 5) * 17 + (row & 15)
        place = jnp.where(slot < count, place, 16)
        total[place] += product

    pair_products(count, right, turned, source, visit)
    for at in range(16):
        total[17 * at + 16] = squares
    keep[...] = total[:half]
    send[...] = total[half:]


def cells_kernel(first, stagger, rows, cols, scalars, left_own, left_other, blocks, out, *rest):
    count, core = scalars[0], scalars[1]
    half = left_own.shape[0]
    arrive, width = None, CHUNK
    if first:
        turned, held, left, sems = rest
        width = FIRST_CHUNK
        pieces = held.shape[0] // width

        def fetch(at):
            piece = pl.ds(at * width, width)
            return pltpu.make_async_copy(blocks.at[piece], held.at[piece], sems.at[at])

        def arrive(at):
            fetch(at).wait()

        for at in range(pieces):
            fetch(at).start()
    else:
        held, (left,) = blocks, rest
    left[pl.ds(core * half, half)] = left_own[...]
    left[pl.ds((1 - core) * half, half)] = left_other[...]
    out[...] = jnp.zeros_like(out)
    side = sum(left[17 * at + 16].astype(jnp.float32) for at in range(16))
    squares = jnp.broadcast_to(jnp.sum(side, axis=1, keepdims=True), side.shape)
    lane = lax.broadcasted_iota(jnp.int32, side.shape, 1)
    packed, exponent = side_of_squares(squares, lane)
    scale = CELL_GAIN * jnp.exp2(-0.5 * exponent)

    def source(slot):
        row = rows[slot]
        return ((row >> 4) & 1) * half + (row >> 5) * 17 + (row & 15)

    def visit(slot, product):
        col = cols[slot]
        place = jnp.where(slot < count, col + (col >> 5), 32)
        out[place] += product * scale
        if first:
            turned[slot] = held[slot].T

    chunks = pair_products(count, left, held, source, visit, width, arrive)
    if first:

        def drain(at, carry):
            arrive(at)
            return carry

        lax.fori_loop(chunks, pieces, drain, 0)
    for at in range(8):
        out[33 * at + 32] = packed
    if stagger:

        @pl.when(core == 1)
        def _():
            pl.delay(stagger)


def send_blocks(sent, values, squares):
    size = sent.shape[0] // 8
    for at, value in enumerate(values):
        rounded = value.astype(jnp.bfloat16)
        for copy in range(8):
            sent[size * copy + at] = rounded
    squares = jnp.sum(squares, axis=1, keepdims=True)
    first = squares.astype(jnp.bfloat16).astype(jnp.float32)
    second = (squares - first).astype(jnp.bfloat16).astype(jnp.float32)
    lane = lax.broadcasted_iota(jnp.int32, (squares.shape[0], LANES), 1)
    side = side_lanes(lane, first, second, squares - first - second).astype(jnp.bfloat16)
    for copy in range(8):
        sent[size * copy + size - 1] = side


def start_kernel(times, sent, raw):
    squares = jnp.zeros(raw.shape[1:], jnp.float32)
    for at in range(raw.shape[0]):
        value = times[:, LANES * at : LANES * (at + 1)]
        raw[at] = value
        squares += value * value
    send_blocks(sent, [times[:, LANES * at : LANES * (at + 1)] for at in range(raw.shape[0])], squares)


def core_kernel(keep, received, out):
    squares = keep[16] + received[16]
    lane = lax.broadcasted_iota(jnp.int32, squares.shape, 1)
    packed, exponent = side_of_squares(squares, lane)
    scale = RAY_GAIN * jnp.exp2(-0.5 * exponent)
    for chip in range(8):
        for at in range(16):
            out[17 * chip + at] = (keep[17 * chip + at] + received[17 * chip + at]) * scale
        out[17 * chip + 16] = packed


def update_kernel(gain, first, last, got, *rest):
    previous, (raw, norm_out, tail) = rest[:-3], rest[-3:]
    size = raw.shape[0] + 1
    weights, total = [], 0.0
    for source in range(8):
        side = got[size * source + size - 1]
        exponent = side[:, 0:1]
        weights.append(jnp.broadcast_to(jnp.exp2(0.5 * exponent) * (1.0 / gain), side.shape))
        total += (side[:, 1:2] + side[:, 2:3]) * (1.0 / 1024.0) * jnp.exp2(exponent)
    norm = jnp.sqrt(jnp.broadcast_to(total, raw.shape[1:]) + NORM_EPS)
    norm_out[...] = norm
    inverse = 1.0 / norm
    weights = [weight * inverse for weight in weights]
    if not first:
        past = norm / previous[1][...]
    squares = jnp.zeros(raw.shape[1:], jnp.float32)
    values = []
    for at in range(size - 1):
        value = got[at] * weights[0]
        for source in range(1, 8):
            value += got[size * source + at] * weights[source]
        if not first:
            value -= previous[0][at] * past
        raw[at] = value
        squares += value * value
        values.append(value)
    if last:
        squares = jnp.broadcast_to(jnp.sum(squares, axis=1, keepdims=True), squares.shape)
        tail[...] = jnp.sum(jnp.where(diagonal(squares.shape), squares, 0.0), axis=0, keepdims=True)
    else:
        send_blocks(tail, [raw[at] for at in range(size - 1)], squares)


def diagonal(shape):
    return lax.broadcasted_iota(jnp.int32, shape, 0) == lax.broadcasted_iota(jnp.int32, shape, 1)


def finish_kernel(sums, raw0, raw1, raw2, alpha0, alpha1, beta0, beta1, beta2, solution_out, scaled_out):
    shape = alpha0.shape
    total = jnp.broadcast_to(jnp.sum(sums[:, 0, :], axis=0, keepdims=True), shape)
    total = jnp.sum(jnp.where(diagonal(shape), total, 0.0), axis=1, keepdims=True)
    alpha2 = jnp.sqrt(jnp.broadcast_to(total, shape) + NORM_EPS)
    phi_bar, rho_bar = beta0[...], alpha0[...]
    step1, turn1, rho_bar, phi_bar = rotation(rho_bar, phi_bar, beta1[...], alpha1[...])
    step2, turn2, rho_bar, phi_bar = rotation(rho_bar, phi_bar, beta2[...], alpha2)
    over0, over1, over2 = 1.0 / alpha0[...], 1.0 / alpha1[...], 1.0 / alpha2
    for at in range(raw0.shape[0]):
        lanes = slice(LANES * at, LANES * (at + 1))
        direction0 = raw0[at] * over0
        direction1 = raw1[at] * over1 - turn1 * direction0
        direction2 = raw2[at] * over2 - turn2 * direction1
        solution_out[:, 0, 0, lanes] = step1 * direction0 + step2 * direction1
        scaled_out[:, 0, 0, lanes] = phi_bar * direction2


def small_call(body, outs, *args):
    return pl.pallas_call(
        body,
        out_shape=outs,
        in_specs=[pl.BlockSpec(memory_space=pltpu.VMEM)] * len(args),
        out_specs=[pl.BlockSpec(memory_space=pltpu.VMEM)] * len(outs),
        compiler_params=pltpu.CompilerParams(vmem_limit_bytes=VMEM_BYTES),
    )(*args)


def kernel_call(body, outs, scratch, tables, vectors, blocks, place=pltpu.VMEM):
    specs = [pl.BlockSpec(memory_space=pltpu.SMEM)] * 3
    specs += [pl.BlockSpec(memory_space=pltpu.VMEM)] * len(vectors)
    specs += [pl.BlockSpec(memory_space=place)]
    slots = blocks.shape[0]
    return pl.pallas_call(
        body,
        out_shape=outs,
        in_specs=specs,
        out_specs=[pl.BlockSpec(memory_space=pltpu.VMEM)] * len(outs),
        scratch_shapes=scratch,
        compiler_params=pltpu.CompilerParams(vmem_limit_bytes=VMEM_BYTES),
        cost_estimate=pl.CostEstimate(
            flops=2 * slots * LANES * LANES * 16, bytes_accessed=slots * LANES * LANES * 2 + (4 << 20), transcendentals=0
        ),
    )(*tables, *vectors, blocks)


def exchange(sent, axes):
    return lax.all_to_all(sent, axes, 0, 0, tiled=True)


def exchange_halves(sent, axes):
    return exchange(sent.astype(jnp.float16), axes).astype(jnp.float32)


def swap_cores(values):
    return lax.ppermute(values, "c", [(0, 1), (1, 0)])


def rotation(rho_bar, phi_bar, beta_norm, alpha_norm):
    rho_new = jnp.sqrt(rho_bar * rho_bar + beta_norm * beta_norm)
    cosine = rho_bar / rho_new
    sine_val = beta_norm / rho_new
    theta_coef = sine_val * alpha_norm
    rho_next = -cosine * alpha_norm
    phi_new = cosine * phi_bar
    phi_next = sine_val * phi_bar
    return (phi_new / rho_new, theta_coef / rho_new, rho_next, phi_next)


def shards(blocks, block_rows, block_cols, counts, travel_times):
    blocks_here = blocks[0, 0]
    core = lax.axis_index("c").astype(jnp.int32)
    tables = (block_rows[0, 0], block_cols[0, 0], jnp.stack([counts[0, 0], core]))
    count_rhs = travel_times.shape[0]
    block = (count_rhs, LANES)
    shape = jax.ShapeDtypeStruct
    rays_sent = shape((8 * 17,) + block, jnp.bfloat16)
    cells_sent = shape((8 * 33,) + block, jnp.bfloat16)
    one = shape(block, jnp.float32)

    def rays_of(sent, turned, left_raw, beta):
        right_full = exchange(sent, DEVICES_OF_ROW)
        keep, send = kernel_call(
            rays_kernel,
            [shape((8 * 17,) + block, jnp.float32)] * 2,
            [pltpu.VMEM((16 * 17,) + block, jnp.float32)],
            tables, (right_full,), turned,
        )
        (both,) = small_call(core_kernel, [shape((8 * 17,) + block, jnp.float32)], keep, swap_cores(send))
        got = exchange_halves(both, CHIPS_OF_COL)
        outs = [shape((16,) + block, jnp.float32), one, rays_sent]
        return small_call(functools.partial(update_kernel, RAY_GAIN, False, False), outs, got, left_raw, beta)

    def cells_of(sent, held, *previous, last=False):
        first = not previous
        left_own = exchange(sent, CHIPS_OF_COL)
        outs = [shape((8 * 33,) + block, jnp.float32)]
        scratch = [pltpu.VMEM((16 * 17,) + block, jnp.bfloat16)]
        if first:
            outs += [shape(held.shape, held.dtype)] * 2
            scratch += [pltpu.SemaphoreType.DMA((held.shape[0] // FIRST_CHUNK,))]
        out, *kept = kernel_call(
            functools.partial(cells_kernel, first, 0 if last else STAGGER),
            outs, scratch, tables, (left_own, swap_cores(left_own)), held,
            pltpu.HBM if first else pltpu.VMEM,
        )
        got = exchange_halves(out, DEVICES_OF_ROW)
        outs = [shape((32,) + block, jnp.float32), one, shape((1, LANES), jnp.float32) if last else cells_sent]
        return (*small_call(functools.partial(update_kernel, CELL_GAIN, first, last), outs, got, *previous), *kept)

    sent, left_raw = small_call(start_kernel, [rays_sent, shape((16,) + block, jnp.float32)], travel_times)
    raw0, beta0, sent, turned, held = cells_of(sent, pltpu.with_memory_space_constraint(blocks_here, pltpu.HBM))
    left_raw, alpha0, sent = rays_of(sent, turned, left_raw, beta0)
    raw1, beta1, sent = cells_of(sent, held, raw0, alpha0)
    left_raw, alpha1, sent = rays_of(sent, turned, left_raw, beta1)
    raw2, beta2, squares = cells_of(sent, held, raw1, alpha1, last=True)
    squares = squares + swap_cores(squares)
    sums = exchange(jnp.broadcast_to(squares, (64, 1, LANES)), DEVICES_OF_ROW + CHIPS_OF_COL)
    flat = shape((count_rhs, 1, 1, 32 * LANES), jnp.float32)
    return small_call(finish_kernel, [flat] * 2, sums, raw0, raw1, raw2, alpha0, alpha1, beta0, beta1, beta2)


def solution(mesh):
    physical = Mesh(mesh.devices.reshape(4, 2, 2, 4, 2), ("z", "xl", "xh", "y", "c"))
    row, col = ("z", "xl"), ("xh", "y", "c")
    placed = (
        P(row, col, None, None, None),
        P(row, col, None),
        P(row, col, None),
        P(row, col),
        P(None, row + col),
    )
    return jax.shard_map(
        shards,
        mesh=physical,
        in_specs=placed,
        out_specs=(P(None, col, row, None), P(None, col, row, None)),
        check_vma=False,
    )
```

```python
import functools

import jax
import jax.numpy as jnp
from jax import lax
from jax.experimental import pallas as pl
from jax.experimental.pallas import tpu as pltpu
from jax.sharding import Mesh, PartitionSpec as P

LANES = 128
NORM_EPS = 1e-06
SQUARES_FLOOR = 1e-30
CELL_GAIN = 4096.0
RAY_GAIN = 2048.0
SLOTS = 192
COUNTS = 2 * SLOTS
FIRST_CHUNK = 32
LIST_CHUNK = 32
STAGGER = 7000
CHIPS_OF_COL = ("xh", "y")
DEVICES_OF_ROW = ("z", "xl")
VMEM_BYTES = 32 << 20


def exponent_of(squares):
    return jnp.ceil(jnp.log2(jnp.maximum(squares, SQUARES_FLOOR)))


def side_lanes(lane, first, second, third):
    return jnp.where(lane == 0, first, jnp.where(lane == 1, second, jnp.where(lane == 2, third, 0.0)))


def side_of_squares(squares, lane):
    exponent = exponent_of(squares)
    fraction = squares * jnp.exp2(-exponent)
    upper = jnp.floor(fraction * 1024.0)
    return side_lanes(lane, exponent, upper, fraction * 1024.0 - upper), exponent


def pair_products(count, vector, held, source, visit, width, arrive, slot_of):
    chunks = (count + (width - 1)) // width

    def chunk(at, carry):
        if arrive is not None:
            arrive(at)
        for step in range(0, width, 2):
            slot = at * width + step
            picked = jnp.concatenate([vector[source(slot)], vector[source(slot + 1)]], axis=0)
            pair = jnp.concatenate([held[slot_of(slot)], held[slot_of(slot + 1)]], axis=1)
            both = lax.dot_general(picked, pair, (((1,), (0,)), ((), ())), preferred_element_type=jnp.float32)
            rhs = both.shape[0] // 2
            visit(slot, both[:rhs, :LANES])
            visit(slot + 1, both[rhs:, LANES:])
        return carry

    lax.fori_loop(0, chunks, chunk, 0)
    return chunks


def sum_of_sides(rows):
    side = sum(row.astype(jnp.float32) for row in rows)
    return jnp.broadcast_to(jnp.sum(side, axis=1, keepdims=True), side.shape)


def listed(table, start, count, vector, held, source, place, spare, out):
    def entry(at):
        return jnp.where(at < count, table[start + at], 0)

    def slot_of(at):
        return entry(at) & 255

    def visit(at, product):
        out[jnp.where(at < count, place(entry(at)), spare)] += product

    pair_products(count, vector, held, lambda at: source(entry(at)), visit, LIST_CHUNK, None, slot_of)


def ray_place(entry):
    row = entry >> 16
    return (row >> 5) * 17 + (row & 15)


def cell_place(entry):
    col = (entry >> 8) & 255
    return col + (col >> 5)


def rays_kernel(other, table, right, turned, out):
    out[...] = jnp.zeros_like(out)
    squares = sum_of_sides([right[33 * at + 32] for at in range(8)])
    start, count = (SLOTS, table[COUNTS + 1]) if other else (0, table[COUNTS])
    listed(table, start, count, right, turned, cell_place, ray_place, 16, out)
    if other:
        packed, exponent = side_of_squares(squares, lax.broadcasted_iota(jnp.int32, squares.shape, 1))
        scale = RAY_GAIN * jnp.exp2(-0.5 * exponent)
        for at in range(out.shape[0]):
            out[at] = out[at] * scale
        squares = packed
    out[16] = squares


def own_cells_kernel(table, left, held, out):
    out[...] = jnp.zeros_like(out)
    listed(table, 0, table[COUNTS], left, held, ray_place, cell_place, 32, out)


def other_cells_kernel(stagger, table, left_own, left, partial_out, held, out):
    out[...] = partial_out[...]
    listed(table, SLOTS, table[COUNTS + 1], left, held, ray_place, cell_place, 32, out)
    squares = sum_of_sides([half[17 * at + 16] for half in (left_own, left) for at in range(8)])
    packed, exponent = side_of_squares(squares, lax.broadcasted_iota(jnp.int32, squares.shape, 1))
    scale = CELL_GAIN * jnp.exp2(-0.5 * exponent)
    for at in range(out.shape[0]):
        out[at] = packed if at % 33 == 32 else out[at] * scale
    if stagger:

        @pl.when(table[COUNTS + 2] == 1)
        def _():
            pl.delay(stagger)


def first_cells_kernel(stagger, rows, cols, scalars, left_own, left_other, blocks, out, turned, held, table, left, sems):
    count, core = scalars[0], scalars[1]
    half = left_own.shape[0]
    pieces = held.shape[0] // FIRST_CHUNK

    def fetch(at):
        piece = pl.ds(at * FIRST_CHUNK, FIRST_CHUNK)
        return pltpu.make_async_copy(blocks.at[piece], held.at[piece], sems.at[at])

    def arrive(at):
        fetch(at).wait()

    for at in range(pieces):
        fetch(at).start()

    def enlist(group, counts):
        own, other = counts
        for step in range(8):
            slot = group * 8 + step
            row = rows[slot]
            filled = jnp.where(slot < count, 1, 0)
            mine = jnp.where(((row >> 4) & 1) == core, filled, 0)
            place = jnp.where(filled == 1, jnp.where(mine == 1, own, SLOTS + other), COUNTS + 3)
            table[place] = slot | (cols[slot] << 8) | (row << 16)
            own, other = own + mine, other + filled - mine
        return own, other

    own, other = lax.fori_loop(0, SLOTS // 8, enlist, (jnp.int32(0), jnp.int32(0)))
    table[COUNTS] = own
    table[COUNTS + 1] = other
    table[COUNTS + 2] = core

    left[pl.ds(core * half, half)] = left_own[...]
    left[pl.ds((1 - core) * half, half)] = left_other[...]
    out[...] = jnp.zeros_like(out)
    squares = sum_of_sides([left[17 * at + 16] for at in range(16)])
    packed, exponent = side_of_squares(squares, lax.broadcasted_iota(jnp.int32, squares.shape, 1))
    scale = CELL_GAIN * jnp.exp2(-0.5 * exponent)

    def source(slot):
        row = rows[slot]
        return ((row >> 4) & 1) * half + (row >> 5) * 17 + (row & 15)

    def visit(slot, product):
        col = cols[slot]
        place = jnp.where(slot < count, col + (col >> 5), 32)
        out[place] += product * scale
        turned[slot] = held[slot].T

    chunks = pair_products(count, left, held, source, visit, FIRST_CHUNK, arrive, lambda slot: slot)

    def drain(at, carry):
        arrive(at)
        return carry

    lax.fori_loop(chunks, pieces, drain, 0)
    for at in range(8):
        out[33 * at + 32] = packed
    if stagger:

        @pl.when(core == 1)
        def _():
            pl.delay(stagger)


def send_blocks(sent, values, squares):
    size = sent.shape[0] // 8
    for at, value in enumerate(values):
        rounded = value.astype(jnp.bfloat16)
        for copy in range(8):
            sent[size * copy + at] = rounded
    squares = jnp.sum(squares, axis=1, keepdims=True)
    first = squares.astype(jnp.bfloat16).astype(jnp.float32)
    second = (squares - first).astype(jnp.bfloat16).astype(jnp.float32)
    lane = lax.broadcasted_iota(jnp.int32, (squares.shape[0], LANES), 1)
    side = side_lanes(lane, first, second, squares - first - second).astype(jnp.bfloat16)
    for copy in range(8):
        sent[size * copy + size - 1] = side


def start_kernel(times, sent, raw):
    squares = jnp.zeros(raw.shape[1:], jnp.float32)
    for at in range(raw.shape[0]):
        value = times[:, LANES * at : LANES * (at + 1)]
        raw[at] = value
        squares += value * value
    send_blocks(sent, [times[:, LANES * at : LANES * (at + 1)] for at in range(raw.shape[0])], squares)


def core_kernel(keep, received, out):
    side = received[16]
    exponent = side[:, 0:1]
    squares = keep[16] + (side[:, 1:2] + side[:, 2:3]) * (1.0 / 1024.0) * jnp.exp2(exponent)
    weight = jnp.broadcast_to(jnp.exp2(0.5 * exponent) * (1.0 / RAY_GAIN), squares.shape)
    packed, exponent = side_of_squares(squares, lax.broadcasted_iota(jnp.int32, squares.shape, 1))
    scale = RAY_GAIN * jnp.exp2(-0.5 * exponent)
    weight = weight * scale
    for chip in range(8):
        for at in range(17 * chip, 17 * chip + 16):
            out[at] = keep[at] * scale + received[at] * weight
        out[17 * chip + 16] = packed


def update_kernel(gain, first, last, got, *rest):
    previous, (norm_out, tail, raw) = rest[:-3], rest[-3:]
    size = raw.shape[0] + 1
    weights, total = [], 0.0
    for source in range(8):
        side = got[size * source + size - 1]
        exponent = side[:, 0:1]
        weights.append(jnp.broadcast_to(jnp.exp2(0.5 * exponent) * (1.0 / gain), side.shape))
        total += (side[:, 1:2] + side[:, 2:3]) * (1.0 / 1024.0) * jnp.exp2(exponent)
    norm = jnp.sqrt(jnp.broadcast_to(total, raw.shape[1:]) + NORM_EPS)
    norm_out[...] = norm
    inverse = 1.0 / norm
    weights = [weight * inverse for weight in weights]
    if not first:
        past = norm / previous[1][...]
    squares = jnp.zeros(raw.shape[1:], jnp.float32)
    values = []
    for at in range(size - 1):
        value = got[at] * weights[0]
        for source in range(1, 8):
            value += got[size * source + at] * weights[source]
        if not first:
            value -= previous[0][at] * past
        raw[at] = value
        squares += value * value
        values.append(value)
    if last:
        squares = jnp.broadcast_to(jnp.sum(squares, axis=1, keepdims=True), squares.shape)
        tail[...] = jnp.sum(jnp.where(diagonal(squares.shape), squares, 0.0), axis=0, keepdims=True)
    else:
        send_blocks(tail, [raw[at] for at in range(size - 1)], squares)


def diagonal(shape):
    return lax.broadcasted_iota(jnp.int32, shape, 0) == lax.broadcasted_iota(jnp.int32, shape, 1)


def finish_kernel(sums, raw0, raw1, raw2, alpha0, alpha1, beta0, beta1, beta2, solution_out, scaled_out):
    shape = alpha0.shape
    total = jnp.broadcast_to(jnp.sum(sums[:, 0, :], axis=0, keepdims=True), shape)
    total = jnp.sum(jnp.where(diagonal(shape), total, 0.0), axis=1, keepdims=True)
    alpha2 = jnp.sqrt(jnp.broadcast_to(total, shape) + NORM_EPS)
    phi_bar, rho_bar = beta0[...], alpha0[...]
    step1, turn1, rho_bar, phi_bar = rotation(rho_bar, phi_bar, beta1[...], alpha1[...])
    step2, turn2, rho_bar, phi_bar = rotation(rho_bar, phi_bar, beta2[...], alpha2)
    over0, over1, over2 = 1.0 / alpha0[...], 1.0 / alpha1[...], 1.0 / alpha2
    for at in range(raw0.shape[0]):
        lanes = slice(LANES * at, LANES * (at + 1))
        direction0 = raw0[at] * over0
        direction1 = raw1[at] * over1 - turn1 * direction0
        direction2 = raw2[at] * over2 - turn2 * direction1
        solution_out[:, 0, 0, lanes] = step1 * direction0 + step2 * direction1
        scaled_out[:, 0, 0, lanes] = phi_bar * direction2


def small_call(body, outs, *args, scratch=()):
    return pl.pallas_call(
        body,
        out_shape=outs,
        in_specs=[pl.BlockSpec(memory_space=pltpu.VMEM)] * len(args),
        out_specs=[pl.BlockSpec(memory_space=pltpu.VMEM)] * len(outs),
        scratch_shapes=scratch,
        compiler_params=pltpu.CompilerParams(vmem_limit_bytes=VMEM_BYTES),
    )(*args)


def kernel_call(body, outs, scalars, *operands, scratch=(), in_hbm=False):
    specs = [pl.BlockSpec(memory_space=pltpu.SMEM)] * len(scalars)
    specs += [pl.BlockSpec(memory_space=pltpu.VMEM)] * (len(operands) - 1)
    specs += [pl.BlockSpec(memory_space=pltpu.HBM if in_hbm else pltpu.VMEM)]
    places = [pltpu.SMEM if out.dtype == jnp.int32 else pltpu.VMEM for out in outs]
    return pl.pallas_call(
        body,
        out_shape=outs,
        in_specs=specs,
        out_specs=[pl.BlockSpec(memory_space=place) for place in places],
        scratch_shapes=scratch,
        compiler_params=pltpu.CompilerParams(vmem_limit_bytes=VMEM_BYTES),
        cost_estimate=pl.CostEstimate(flops=10**9, bytes_accessed=4 << 20, transcendentals=0),
    )(*scalars, *operands)


def exchange(sent, axes):
    return lax.all_to_all(sent, axes, 0, 0, tiled=True)


def exchange_halves(sent, axes):
    return exchange(sent.astype(jnp.float16), axes).astype(jnp.float32)


def swap_cores(values):
    return lax.ppermute(values, "c", [(0, 1), (1, 0)])


def rotation(rho_bar, phi_bar, beta_norm, alpha_norm):
    rho_new = jnp.sqrt(rho_bar * rho_bar + beta_norm * beta_norm)
    cosine = rho_bar / rho_new
    sine_val = beta_norm / rho_new
    theta_coef = sine_val * alpha_norm
    rho_next = -cosine * alpha_norm
    phi_new = cosine * phi_bar
    phi_next = sine_val * phi_bar
    return (phi_new / rho_new, theta_coef / rho_new, rho_next, phi_next)


def shards(blocks, block_rows, block_cols, counts, travel_times):
    blocks_here = blocks[0, 0]
    core = lax.axis_index("c").astype(jnp.int32)
    tables = (block_rows[0, 0], block_cols[0, 0], jnp.stack([counts[0, 0], core]))
    count_rhs = travel_times.shape[0]
    block = (count_rhs, LANES)
    shape = jax.ShapeDtypeStruct
    rays_sent = shape((8 * 17,) + block, jnp.bfloat16)
    cells_sent = shape((8 * 33,) + block, jnp.bfloat16)
    one = shape(block, jnp.float32)

    rays_part = [shape((8 * 17,) + block, jnp.float32)]
    cells_part = [shape((8 * 33,) + block, jnp.float32)]

    def rays_of(sent, table, turned, left_raw, beta, last=False):
        right = exchange(sent, DEVICES_OF_ROW)
        (send,) = kernel_call(functools.partial(rays_kernel, True), rays_part, [table], right, turned)
        received = swap_cores(send.astype(jnp.float16))
        (keep,) = kernel_call(functools.partial(rays_kernel, False), rays_part, [table], right, turned)
        (both,) = small_call(core_kernel, rays_part, keep, received.astype(jnp.float32))
        got = exchange_halves(both, CHIPS_OF_COL)
        body = functools.partial(update_kernel, RAY_GAIN, False, False)
        raw = shape((16,) + block, jnp.float32)
        if last:
            return small_call(body, [one, rays_sent], got, left_raw, beta, scratch=[pltpu.VMEM(raw.shape, raw.dtype)])
        return small_call(body, [one, rays_sent, raw], got, left_raw, beta)

    def cells_of(sent, table, held, *previous, last=False):
        left_own = exchange(sent, CHIPS_OF_COL)
        left_other = swap_cores(left_own)
        (out,) = kernel_call(own_cells_kernel, cells_part, [table], left_own, held)
        body = functools.partial(other_cells_kernel, 0 if last else STAGGER)
        (out,) = kernel_call(body, cells_part, [table], left_own, left_other, out, held)
        got = exchange_halves(out, DEVICES_OF_ROW)
        outs = [one, shape((1, LANES), jnp.float32) if last else cells_sent, shape((32,) + block, jnp.float32)]
        return small_call(functools.partial(update_kernel, CELL_GAIN, False, last), outs, got, *previous)

    def first_cells_of(sent):
        left_own = exchange(sent, CHIPS_OF_COL)
        outs = cells_part + [shape(blocks_here.shape, jnp.bfloat16)] * 2 + [shape((COUNTS + 16,), jnp.int32)]
        scratch = [
            pltpu.VMEM((16 * 17,) + block, jnp.bfloat16),
            pltpu.SemaphoreType.DMA((SLOTS // FIRST_CHUNK,)),
        ]
        out, turned, held, table = kernel_call(
            functools.partial(first_cells_kernel, STAGGER),
            outs, tables, left_own, swap_cores(left_own),
            pltpu.with_memory_space_constraint(blocks_here, pltpu.HBM),
            scratch=scratch, in_hbm=True,
        )
        got = exchange_halves(out, DEVICES_OF_ROW)
        outs = [one, cells_sent, shape((32,) + block, jnp.float32)]
        return (*small_call(functools.partial(update_kernel, CELL_GAIN, True, False), outs, got), turned, held, table)

    sent, left_raw = small_call(start_kernel, [rays_sent, shape((16,) + block, jnp.float32)], travel_times)
    beta0, sent, raw0, turned, held, table = first_cells_of(sent)
    alpha0, sent, left_raw = rays_of(sent, table, turned, left_raw, beta0)
    beta1, sent, raw1 = cells_of(sent, table, held, raw0, alpha0)
    alpha1, sent = rays_of(sent, table, turned, left_raw, beta1, last=True)
    beta2, squares, raw2 = cells_of(sent, table, held, raw1, alpha1, last=True)
    squares = squares + swap_cores(squares)
    sums = exchange(jnp.broadcast_to(squares, (64, 1, LANES)), DEVICES_OF_ROW + CHIPS_OF_COL)
    flat = shape((count_rhs, 1, 1, 32 * LANES), jnp.float32)
    return small_call(finish_kernel, [flat] * 2, sums, raw0, raw1, raw2, alpha0, alpha1, beta0, beta1, beta2)


def solution(mesh):
    physical = Mesh(mesh.devices.reshape(4, 2, 2, 4, 2), ("z", "xl", "xh", "y", "c"))
    row, col = ("z", "xl"), ("xh", "y", "c")
    placed = (
        P(row, col, None, None, None),
        P(row, col, None),
        P(row, col, None),
        P(row, col),
        P(None, row + col),
    )
    return jax.shard_map(
        shards,
        mesh=physical,
        in_specs=placed,
        out_specs=(P(None, col, row, None), P(None, col, row, None)),
        check_vma=False,
    )
```

```python
import functools

import jax
import jax.numpy as jnp
from jax import lax
from jax.experimental import pallas as pl
from jax.experimental.pallas import tpu as pltpu
from jax.sharding import Mesh, PartitionSpec as P

LANES = 128
NORM_EPS = 1e-06
SQUARES_FLOOR = 1e-30
CELL_GAIN = 4096.0
RAY_GAIN = 2048.0
SLOTS = 192
COUNTS = 2 * SLOTS
FIRST_CHUNK = 32
LIST_CHUNK = 64
STAGGER = 7000
CHIPS_OF_COL = ("xh", "y")
DEVICES_OF_ROW = ("z", "xl")
VMEM_BYTES = 32 << 20


def exponent_of(squares):
    return jnp.ceil(jnp.log2(jnp.maximum(squares, SQUARES_FLOOR)))


def side_lanes(lane, first, second, third):
    return jnp.where(lane == 0, first, jnp.where(lane == 1, second, jnp.where(lane == 2, third, 0.0)))


def side_of_squares(squares, lane):
    exponent = exponent_of(squares)
    fraction = squares * jnp.exp2(-exponent)
    upper = jnp.floor(fraction * 1024.0)
    return side_lanes(lane, exponent, upper, fraction * 1024.0 - upper), exponent


def pair_products(count, vector, held, source, visit, width, arrive, slot_of):
    chunks = (count + (width - 1)) // width

    def chunk(at, carry):
        if arrive is not None:
            arrive(at)
        for step in range(0, width, 2):
            slot = at * width + step
            picked = jnp.concatenate([vector[source(slot)], vector[source(slot + 1)]], axis=0)
            pair = jnp.concatenate([held[slot_of(slot)], held[slot_of(slot + 1)]], axis=1)
            both = lax.dot_general(picked, pair, (((1,), (0,)), ((), ())), preferred_element_type=jnp.float32)
            rhs = both.shape[0] // 2
            visit(slot, both[:rhs, :LANES])
            visit(slot + 1, both[rhs:, LANES:])
        return carry

    lax.fori_loop(0, chunks, chunk, 0)
    return chunks


def sum_of_sides(rows):
    side = sum(row.astype(jnp.float32) for row in rows)
    return jnp.broadcast_to(jnp.sum(side, axis=1, keepdims=True), side.shape)


def listed(table, start, count, vector, held, source, place, spare, out):
    def entry(at):
        return jnp.where(at < count, table[start + at], 0)

    def slot_of(at):
        return entry(at) & 255

    def visit(at, product):
        out[jnp.where(at < count, place(entry(at)), spare)] += product

    pair_products(count, vector, held, lambda at: source(entry(at)), visit, LIST_CHUNK, None, slot_of)


def ray_place(entry):
    row = entry >> 16
    return (row >> 5) * 17 + (row & 15)


def cell_place(entry):
    col = (entry >> 8) & 255
    return col + (col >> 5)


def rays_kernel(other, table, right, turned, out):
    out[...] = jnp.zeros_like(out)
    squares = sum_of_sides([right[33 * at + 32] for at in range(8)])
    start, count = (SLOTS, table[COUNTS + 1]) if other else (0, table[COUNTS])
    listed(table, start, count, right, turned, cell_place, ray_place, 16, out)
    if other:
        packed, exponent = side_of_squares(squares, lax.broadcasted_iota(jnp.int32, squares.shape, 1))
        scale = RAY_GAIN * jnp.exp2(-0.5 * exponent)
        for at in range(out.shape[0]):
            out[at] = out[at] * scale
        squares = packed
    out[16] = squares


def own_cells_kernel(table, left, held, out):
    out[...] = jnp.zeros_like(out)
    listed(table, 0, table[COUNTS], left, held, ray_place, cell_place, 32, out)


def other_cells_kernel(stagger, table, left_own, left, partial_out, held, out):
    out[...] = partial_out[...]
    listed(table, SLOTS, table[COUNTS + 1], left, held, ray_place, cell_place, 32, out)
    squares = sum_of_sides([half[17 * at + 16] for half in (left_own, left) for at in range(8)])
    packed, exponent = side_of_squares(squares, lax.broadcasted_iota(jnp.int32, squares.shape, 1))
    scale = CELL_GAIN * jnp.exp2(-0.5 * exponent)
    for at in range(out.shape[0]):
        out[at] = packed if at % 33 == 32 else out[at] * scale
    if stagger:

        @pl.when(table[COUNTS + 2] == 1)
        def _():
            pl.delay(stagger)


def first_cells_kernel(stagger, rows, cols, scalars, left_own, left_other, blocks, out, turned, held, table, left, sems):
    count, core = scalars[0], scalars[1]
    half = left_own.shape[0]
    pieces = held.shape[0] // FIRST_CHUNK

    def fetch(at):
        piece = pl.ds(at * FIRST_CHUNK, FIRST_CHUNK)
        return pltpu.make_async_copy(blocks.at[piece], held.at[piece], sems.at[at])

    def arrive(at):
        fetch(at).wait()

    for at in range(pieces):
        fetch(at).start()

    def enlist(group, counts):
        own, other = counts
        for step in range(8):
            slot = group * 8 + step
            row = rows[slot]
            filled = jnp.where(slot < count, 1, 0)
            mine = jnp.where(((row >> 4) & 1) == core, filled, 0)
            place = jnp.where(filled == 1, jnp.where(mine == 1, own, SLOTS + other), COUNTS + 3)
            table[place] = slot | (cols[slot] << 8) | (row << 16)
            own, other = own + mine, other + filled - mine
        return own, other

    own, other = lax.fori_loop(0, SLOTS // 8, enlist, (jnp.int32(0), jnp.int32(0)))
    table[COUNTS] = own
    table[COUNTS + 1] = other
    table[COUNTS + 2] = core

    left[pl.ds(core * half, half)] = left_own[...]
    left[pl.ds((1 - core) * half, half)] = left_other[...]
    out[...] = jnp.zeros_like(out)
    squares = sum_of_sides([left[17 * at + 16] for at in range(16)])
    packed, exponent = side_of_squares(squares, lax.broadcasted_iota(jnp.int32, squares.shape, 1))
    scale = CELL_GAIN * jnp.exp2(-0.5 * exponent)

    def source(slot):
        row = rows[slot]
        return ((row >> 4) & 1) * half + (row >> 5) * 17 + (row & 15)

    def visit(slot, product):
        col = cols[slot]
        place = jnp.where(slot < count, col + (col >> 5), 32)
        out[place] += product * scale
        turned[slot] = held[slot].T

    chunks = pair_products(count, left, held, source, visit, FIRST_CHUNK, arrive, lambda slot: slot)

    def drain(at, carry):
        arrive(at)
        return carry

    lax.fori_loop(chunks, pieces, drain, 0)
    for at in range(8):
        out[33 * at + 32] = packed
    if stagger:

        @pl.when(core == 1)
        def _():
            pl.delay(stagger)


def send_blocks(sent, values, squares):
    size = sent.shape[0] // 8
    for at, value in enumerate(values):
        rounded = value.astype(jnp.bfloat16)
        for copy in range(8):
            sent[size * copy + at] = rounded
    squares = jnp.sum(squares, axis=1, keepdims=True)
    first = squares.astype(jnp.bfloat16).astype(jnp.float32)
    second = (squares - first).astype(jnp.bfloat16).astype(jnp.float32)
    lane = lax.broadcasted_iota(jnp.int32, (squares.shape[0], LANES), 1)
    side = side_lanes(lane, first, second, squares - first - second).astype(jnp.bfloat16)
    for copy in range(8):
        sent[size * copy + size - 1] = side


def start_kernel(times, sent, raw):
    squares = jnp.zeros(raw.shape[1:], jnp.float32)
    for at in range(raw.shape[0]):
        value = times[:, LANES * at : LANES * (at + 1)]
        raw[at] = value
        squares += value * value
    send_blocks(sent, [times[:, LANES * at : LANES * (at + 1)] for at in range(raw.shape[0])], squares)


def core_kernel(keep, received, out):
    side = received[16]
    exponent = side[:, 0:1]
    squares = keep[16] + (side[:, 1:2] + side[:, 2:3]) * (1.0 / 1024.0) * jnp.exp2(exponent)
    weight = jnp.broadcast_to(jnp.exp2(0.5 * exponent) * (1.0 / RAY_GAIN), squares.shape)
    packed, exponent = side_of_squares(squares, lax.broadcasted_iota(jnp.int32, squares.shape, 1))
    scale = RAY_GAIN * jnp.exp2(-0.5 * exponent)
    weight = weight * scale
    for chip in range(8):
        for at in range(17 * chip, 17 * chip + 16):
            out[at] = keep[at] * scale + received[at] * weight
        out[17 * chip + 16] = packed


def update_kernel(gain, first, last, got, *rest):
    previous, (norm_out, tail, raw) = rest[:-3], rest[-3:]
    size = raw.shape[0] + 1
    weights, total = [], 0.0
    for source in range(8):
        side = got[size * source + size - 1]
        exponent = side[:, 0:1]
        weights.append(jnp.broadcast_to(jnp.exp2(0.5 * exponent) * (1.0 / gain), side.shape))
        total += (side[:, 1:2] + side[:, 2:3]) * (1.0 / 1024.0) * jnp.exp2(exponent)
    norm = jnp.sqrt(jnp.broadcast_to(total, raw.shape[1:]) + NORM_EPS)
    norm_out[...] = norm
    inverse = 1.0 / norm
    weights = [weight * inverse for weight in weights]
    if not first:
        past = norm / previous[1][...]
    squares = jnp.zeros(raw.shape[1:], jnp.float32)
    values = []
    for at in range(size - 1):
        value = got[at] * weights[0]
        for source in range(1, 8):
            value += got[size * source + at] * weights[source]
        if not first:
            value -= previous[0][at] * past
        raw[at] = value
        squares += value * value
        values.append(value)
    if last:
        squares = jnp.broadcast_to(jnp.sum(squares, axis=1, keepdims=True), squares.shape)
        tail[...] = jnp.sum(jnp.where(diagonal(squares.shape), squares, 0.0), axis=0, keepdims=True)
    else:
        send_blocks(tail, [raw[at] for at in range(size - 1)], squares)


def diagonal(shape):
    return lax.broadcasted_iota(jnp.int32, shape, 0) == lax.broadcasted_iota(jnp.int32, shape, 1)


def finish_kernel(sums, raw0, raw1, raw2, alpha0, alpha1, beta0, beta1, beta2, solution_out, scaled_out):
    shape = alpha0.shape
    total = jnp.broadcast_to(jnp.sum(sums[:, 0, :], axis=0, keepdims=True), shape)
    total = jnp.sum(jnp.where(diagonal(shape), total, 0.0), axis=1, keepdims=True)
    alpha2 = jnp.sqrt(jnp.broadcast_to(total, shape) + NORM_EPS)
    phi_bar, rho_bar = beta0[...], alpha0[...]
    step1, turn1, rho_bar, phi_bar = rotation(rho_bar, phi_bar, beta1[...], alpha1[...])
    step2, turn2, rho_bar, phi_bar = rotation(rho_bar, phi_bar, beta2[...], alpha2)
    over0, over1, over2 = 1.0 / alpha0[...], 1.0 / alpha1[...], 1.0 / alpha2
    for at in range(raw0.shape[0]):
        lanes = slice(LANES * at, LANES * (at + 1))
        direction0 = raw0[at] * over0
        direction1 = raw1[at] * over1 - turn1 * direction0
        direction2 = raw2[at] * over2 - turn2 * direction1
        solution_out[:, 0, 0, lanes] = step1 * direction0 + step2 * direction1
        scaled_out[:, 0, 0, lanes] = phi_bar * direction2


def small_call(body, outs, *args, scratch=()):
    return pl.pallas_call(
        body,
        out_shape=outs,
        in_specs=[pl.BlockSpec(memory_space=pltpu.VMEM)] * len(args),
        out_specs=[pl.BlockSpec(memory_space=pltpu.VMEM)] * len(outs),
        scratch_shapes=scratch,
        compiler_params=pltpu.CompilerParams(vmem_limit_bytes=VMEM_BYTES),
    )(*args)


def kernel_call(body, outs, scalars, *operands, scratch=(), in_hbm=False):
    specs = [pl.BlockSpec(memory_space=pltpu.SMEM)] * len(scalars)
    specs += [pl.BlockSpec(memory_space=pltpu.VMEM)] * (len(operands) - 1)
    specs += [pl.BlockSpec(memory_space=pltpu.HBM if in_hbm else pltpu.VMEM)]
    places = [pltpu.SMEM if out.dtype == jnp.int32 else pltpu.VMEM for out in outs]
    return pl.pallas_call(
        body,
        out_shape=outs,
        in_specs=specs,
        out_specs=[pl.BlockSpec(memory_space=place) for place in places],
        scratch_shapes=scratch,
        compiler_params=pltpu.CompilerParams(vmem_limit_bytes=VMEM_BYTES),
        cost_estimate=pl.CostEstimate(flops=10**9, bytes_accessed=4 << 20, transcendentals=0),
    )(*scalars, *operands)


def exchange(sent, axes):
    return lax.all_to_all(sent, axes, 0, 0, tiled=True)


def exchange_halves(sent, axes):
    return exchange(sent.astype(jnp.float16), axes).astype(jnp.float32)


def swap_cores(values):
    return lax.ppermute(values, "c", [(0, 1), (1, 0)])


def rotation(rho_bar, phi_bar, beta_norm, alpha_norm):
    rho_new = jnp.sqrt(rho_bar * rho_bar + beta_norm * beta_norm)
    cosine = rho_bar / rho_new
    sine_val = beta_norm / rho_new
    theta_coef = sine_val * alpha_norm
    rho_next = -cosine * alpha_norm
    phi_new = cosine * phi_bar
    phi_next = sine_val * phi_bar
    return (phi_new / rho_new, theta_coef / rho_new, rho_next, phi_next)


def shards(blocks, block_rows, block_cols, counts, travel_times):
    blocks_here = blocks[0, 0]
    core = lax.axis_index("c").astype(jnp.int32)
    tables = (block_rows[0, 0], block_cols[0, 0], jnp.stack([counts[0, 0], core]))
    count_rhs = travel_times.shape[0]
    block = (count_rhs, LANES)
    shape = jax.ShapeDtypeStruct
    rays_sent = shape((8 * 17,) + block, jnp.bfloat16)
    cells_sent = shape((8 * 33,) + block, jnp.bfloat16)
    one = shape(block, jnp.float32)

    rays_part = [shape((8 * 17,) + block, jnp.float32)]
    cells_part = [shape((8 * 33,) + block, jnp.float32)]

    def rays_of(sent, table, turned, left_raw, beta, last=False):
        right = exchange(sent, DEVICES_OF_ROW)
        (send,) = kernel_call(functools.partial(rays_kernel, True), rays_part, [table], right, turned)
        received = swap_cores(send.astype(jnp.float16))
        (keep,) = kernel_call(functools.partial(rays_kernel, False), rays_part, [table], right, turned)
        (both,) = small_call(core_kernel, rays_part, keep, received.astype(jnp.float32))
        got = exchange_halves(both, CHIPS_OF_COL)
        body = functools.partial(update_kernel, RAY_GAIN, False, False)
        raw = shape((16,) + block, jnp.float32)
        if last:
            return small_call(body, [one, rays_sent], got, left_raw, beta, scratch=[pltpu.VMEM(raw.shape, raw.dtype)])
        return small_call(body, [one, rays_sent, raw], got, left_raw, beta)

    def cells_of(sent, table, held, *previous, last=False):
        left_own = exchange(sent, CHIPS_OF_COL)
        left_other = swap_cores(left_own)
        (out,) = kernel_call(own_cells_kernel, cells_part, [table], left_own, held)
        body = functools.partial(other_cells_kernel, 0 if last else STAGGER)
        (out,) = kernel_call(body, cells_part, [table], left_own, left_other, out, held)
        got = exchange_halves(out, DEVICES_OF_ROW)
        outs = [one, shape((1, LANES), jnp.float32) if last else cells_sent, shape((32,) + block, jnp.float32)]
        return small_call(functools.partial(update_kernel, CELL_GAIN, False, last), outs, got, *previous)

    def first_cells_of(sent):
        left_own = exchange(sent, CHIPS_OF_COL)
        outs = cells_part + [shape(blocks_here.shape, jnp.bfloat16)] * 2 + [shape((COUNTS + 16,), jnp.int32)]
        scratch = [
            pltpu.VMEM((16 * 17,) + block, jnp.bfloat16),
            pltpu.SemaphoreType.DMA((SLOTS // FIRST_CHUNK,)),
        ]
        out, turned, held, table = kernel_call(
            functools.partial(first_cells_kernel, STAGGER),
            outs, tables, left_own, swap_cores(left_own),
            pltpu.with_memory_space_constraint(blocks_here, pltpu.HBM),
            scratch=scratch, in_hbm=True,
        )
        got = exchange_halves(out, DEVICES_OF_ROW)
        outs = [one, cells_sent, shape((32,) + block, jnp.float32)]
        return (*small_call(functools.partial(update_kernel, CELL_GAIN, True, False), outs, got), turned, held, table)

    sent, left_raw = small_call(start_kernel, [rays_sent, shape((16,) + block, jnp.float32)], travel_times)
    beta0, sent, raw0, turned, held, table = first_cells_of(sent)
    alpha0, sent, left_raw = rays_of(sent, table, turned, left_raw, beta0)
    beta1, sent, raw1 = cells_of(sent, table, held, raw0, alpha0)
    alpha1, sent = rays_of(sent, table, turned, left_raw, beta1, last=True)
    beta2, squares, raw2 = cells_of(sent, table, held, raw1, alpha1, last=True)
    squares = squares + swap_cores(squares)
    sums = exchange(jnp.broadcast_to(squares, (64, 1, LANES)), DEVICES_OF_ROW + CHIPS_OF_COL)
    flat = shape((count_rhs, 1, 1, 32 * LANES), jnp.float32)
    return small_call(finish_kernel, [flat] * 2, sums, raw0, raw1, raw2, alpha0, alpha1, beta0, beta1, beta2)


def solution(mesh):
    physical = Mesh(mesh.devices.reshape(4, 2, 2, 4, 2), ("z", "xl", "xh", "y", "c"))
    row, col = ("z", "xl"), ("xh", "y", "c")
    placed = (
        P(row, col, None, None, None),
        P(row, col, None),
        P(row, col, None),
        P(row, col),
        P(None, row + col),
    )
    return jax.shard_map(
        shards,
        mesh=physical,
        in_specs=placed,
        out_specs=(P(None, col, row, None), P(None, col, row, None)),
        check_vma=False,
    )
```
